32 devices in a mesh: groups: 2 (over y), ctx: 4 (over z), head: 4 (over x, core).
Axes of the slice: x: 2, y: 2, z: 4, core: 2. Of those that a mesh axis runs over, the one named last changes fastest.
Arguments:
- queries: bfloat16 [4096, 4096], P(('groups', 'ctx'), 'head'), parts along dimension 0, may hold values from -40 to 40
- keys: bfloat16 [4096, 4096], P(('groups', 'ctx'), 'head'), parts along dimension 0, may hold values from -4 to 4
- values: bfloat16 [4096, 4096], P(('groups', 'ctx'), 'head'), parts along dimension 0, may hold values from -40 to 40
- log_decay: bfloat16 [4096, 32], P(('groups', 'ctx'), 'head'), parts along dimension 0, may hold values from -1.6 to 0
- arrival_positions: int32 [4096], P(('groups', 'ctx')), parts along dimension 0, may hold values from 0 to 2047, as said below
- prompt_lengths: int32 [8], P('groups'), parts along dimension 0, may hold values from 1 to 1024, 2048 in all
- norm_gain: float32 [4096], P('head'), may hold values from 0.5 to 2
- out_weight: bfloat16 [4096, 6144], P(None, 'head'), may hold values from -0.09375 to 0.09375
Outputs:
- layer_out: bfloat16 [4096, 6144], P(('groups', 'ctx'), 'head'), parts along dimension 0
The draws below stay inside these ranges and needn't reach their ends.
There are 2 independent parts, one for each index of `groups`. The reference program is written for one: setup_inputs(seed, part) draws one part's arguments, and reference() takes and returns one part's arrays. A program takes and returns all parts, laid end to end along the dimension named above; an argument that names none is the same for every part. Nothing has to cross between parts.
Inputs may be any that keep to these rules, and one draw needn't show every extreme that they name: `arrival_positions`: each packed position appears once. The rows that one arrival device holds of one owner are one run of consecutive positions, of 64 or 192 rows, and every arrival device holds such a run of every owner. `prompt_lengths`: they sum to 2048; the longest is exactly 1024.
All inputs are finite; a program needn't handle non-finite values.
Results may differ from the reference program's by a relative error of at most 0.013.
Values may be sent and summed in bfloat16 or wider, within the bound.
A program may use at most 64 MiB of HBM per device.

```python
import math
import jax
import jax.numpy as jnp
import numpy as np
from jax import lax

D = 6144
HEAD_TOTAL = 32
DH = 128
TOK_DEV = 512
PROMPTS = 4
TOKENS = 2048


def arrival_layout(key):
    owners = TOKENS // TOK_DEV
    unit_rows = TOK_DEV // (2 * owners)
    key_size, key_shift, key_order = jax.random.split(jax.random.fold_in(key, 11), 3)
    base_units = jnp.where(jnp.arange(owners) < owners // 2, 1, 3)
    piece_sizes = unit_rows * base_units[jax.random.permutation(key_size, owners)]
    offsets = jnp.cumsum(piece_sizes) - piece_sizes
    shifts = jax.random.permutation(key_shift, owners)
    orders = jax.vmap(lambda sub_key: jax.random.permutation(sub_key, owners))(jax.random.split(key_order, owners))
    slot_sizes = piece_sizes[orders]
    slot_ends = jnp.cumsum(slot_sizes, axis=1)
    slot_starts = slot_ends - slot_sizes
    row_line = jnp.arange(TOK_DEV)
    slot_of = jnp.sum((row_line[None, :, None] >= slot_ends[:, None, :]).astype(jnp.int32), axis=2)
    piece_of = jnp.take_along_axis(orders, slot_of, axis=1)
    within = row_line[None, :] - jnp.take_along_axis(slot_starts, slot_of, axis=1)
    owner_of = (jnp.arange(owners)[:, None] - shifts[piece_of]) % owners
    return (owner_of * TOK_DEV + offsets[piece_of] + within).reshape(-1).astype(jnp.int32)


def draw_arrival_positions(key, part):
    return arrival_layout(key)


def draw_log_decay(key, part):
    positions = arrival_layout(key)
    random_key_ordering, random_key_quick, random_key_block, random_key_jitter, random_key_location, random_key_cluster = jax.random.split(jax.random.fold_in(key, 23), 6)
    rank_line = jax.random.permutation(random_key_ordering, HEAD_TOTAL)
    fast_heads = HEAD_TOTAL // 2
    rough_low = 0.5
    rough_high = 1.5
    fast_rate = jnp.exp(jax.random.uniform(random_key_quick, (HEAD_TOTAL,), jnp.float32, math.log(1.0 / 50.0), math.log(1.0 / 30.0)))
    head_decay_rate = jnp.where(rank_line < fast_heads, fast_rate, 0.5 / TOKENS)
    owners = TOKENS // TOK_DEV
    block_multiplier = jnp.repeat(jnp.exp(jax.random.uniform(random_key_block, (owners, HEAD_TOTAL), jnp.float32, math.log(0.5), math.log(2.0))), TOK_DEV, axis=0)
    jitter_level = jax.random.uniform(random_key_jitter, (TOKENS, HEAD_TOTAL), jnp.float32, rough_low, rough_high)
    spots = jax.random.randint(random_key_location, (2, HEAD_TOTAL), 0, TOKENS)
    cluster_length = jax.random.uniform(random_key_cluster, (2, HEAD_TOTAL), jnp.float32, math.log(0.5), math.log(0.8))
    match_mask = jnp.arange(TOKENS)[:, None, None] == spots[None, :, :]
    prompt_clusters = jnp.sum(jnp.where(match_mask, cluster_length[None, :, :], 0.0), axis=1)
    packed_tensors = -head_decay_rate[None, :] * block_multiplier * jitter_level + prompt_clusters
    return packed_tensors[positions].astype(jnp.bfloat16)


def draw_queries(key, part):
    key_value, key_scale = jax.random.split(jax.random.fold_in(key, 31), 2)
    base_values = jax.random.truncated_normal(key_value, -4.0, 4.0, (TOKENS, HEAD_TOTAL * DH), jnp.float32)
    top_scale = 10.0
    row_scale = jnp.exp(jax.random.uniform(key_scale, (TOKENS, 1), jnp.float32, 0.0, math.log(top_scale)))
    return (base_values * row_scale).astype(jnp.bfloat16)


def draw_values(key, part):
    key_value, key_scale = jax.random.split(jax.random.fold_in(key, 41), 2)
    base_values = jax.random.truncated_normal(key_value, -4.0, 4.0, (TOKENS, HEAD_TOTAL * DH), jnp.float32)
    column_scale = jnp.exp(jax.random.uniform(key_scale, (1, HEAD_TOTAL * DH), jnp.float32, 0.0, math.log(10.0)))
    return (base_values * column_scale).astype(jnp.bfloat16)


def block_levels(own_key, dims, cuts, least, top_value):
    level = 1.0
    for dim, parts in cuts:
        heights = jax.random.uniform(jax.random.fold_in(jax.random.fold_in(own_key, 6), dim), (parts,), jnp.float32, least / len(cuts), top_value / len(cuts))
        level = level * jnp.repeat(jnp.exp(heights), dims[dim] // parts).reshape((-1,) + (1,) * (len(dims) - 1 - dim))
    return level


def split_up(number_of, total, bound, lean):
    weights = [(1 << 20) // math.isqrt(standing ** lean) + 1 for standing in range(2, number_of + 1)]
    rest, holding = total - bound - (number_of - 1), [1] * (number_of - 1)
    while rest > 0:
        candidates = [i for i in range(number_of - 1) if holding[i] < bound]
        pool, budget = sum([weights[i] for i in candidates]), rest
        for i in candidates:
            addition = min(bound - holding[i], max(1, budget * weights[i] // pool), rest)
            holding[i] = holding[i] + addition
            rest = rest - addition
    return np.array([bound] + holding)


def ragged_sizes(key, count, total, bound, slope):
    if count == 2:
        one = jax.random.randint(key, (), max(1, total - bound), min(bound, total - 1) + 1)
        return jnp.stack([one, total - one])
    sizes = jnp.asarray(split_up(count, total, bound, slope), jnp.int32)
    pairs = (count - 1) // 2
    donor, sink = sizes[1:1 + 2 * pairs:2], sizes[2:2 + 2 * pairs:2]
    margin = jnp.minimum(donor - 1, bound - sink)
    passed = jax.random.randint(jax.random.fold_in(key, 1), (pairs,), 0, 1 << 20) % (margin + 1)
    sizes = sizes.at[1:1 + 2 * pairs:2].set(donor - passed).at[2:2 + 2 * pairs:2].set(sink + passed)
    return sizes[jax.random.permutation(jax.random.fold_in(key, 2), count)]


def scatter_about(stream_key, dims, scale, limit, cuts=(), kind=jnp.bfloat16):
    factor_of = block_levels(stream_key, dims, cuts, -0.22, 0.18) if cuts else 1.0
    result = jax.random.normal(stream_key, dims, jnp.float32) * scale * factor_of
    return jnp.minimum(jnp.maximum(result, -limit), limit).astype(kind)


def setup_inputs(seed: int = 0, part: int = 0) -> dict:
    arg_keys = jax.random.split(jax.random.key(seed), 9)
    part_keys = jax.random.split(jax.random.fold_in(arg_keys[8], part), 9)
    queries = draw_queries(jax.random.fold_in(jax.random.fold_in(arg_keys[8], part), 71), part)
    keys = scatter_about(part_keys[1], (TOKENS, HEAD_TOTAL * DH), 1.0, 4.0, ((0, 4), (1, 4)))
    values = draw_values(jax.random.fold_in(jax.random.fold_in(arg_keys[8], part), 71), part)
    log_decay = draw_log_decay(jax.random.fold_in(jax.random.fold_in(arg_keys[8], part), 71), part)
    arrival_positions = draw_arrival_positions(jax.random.fold_in(jax.random.fold_in(arg_keys[8], part), 71), part)
    prompt_lengths = ragged_sizes(part_keys[5], PROMPTS, TOKENS, TOKENS // 2, 2).astype(jnp.int32)
    norm_gain = jnp.clip(jnp.exp(math.log(2.0) - 1.3862944 * jax.random.uniform(arg_keys[6], (HEAD_TOTAL * DH,), jnp.float32) ** block_levels(arg_keys[6], (HEAD_TOTAL * DH,), ((0, 4),), -0.2, 0.2)), 0.5, 2.0)
    out_weight = scatter_about(arg_keys[7], (HEAD_TOTAL * DH, D), (HEAD_TOTAL * DH) ** -0.5, 0.09375, ((1, 4),))
    return dict(queries=queries, keys=keys, values=values, log_decay=log_decay, arrival_positions=arrival_positions, prompt_lengths=prompt_lengths, norm_gain=norm_gain, out_weight=out_weight)


def block_step(carry, block):
    run_state, last_cum, last_seg = carry
    block_q, block_k, block_v, block_cum, block_seg = block
    query_f = block_q.astype(jnp.float32)
    key_f = block_k.astype(jnp.float32)
    value_f = block_v.astype(jnp.float32)
    linked = block_seg == last_seg
    reach_back = jnp.where(linked[:, None], jnp.exp(block_cum - last_cum[None, :]), 0.0)
    earlier = jnp.einsum('thd,hde->the', query_f, run_state, precision=lax.Precision.HIGHEST) * reach_back[:, :, None]
    block_rows = block_seg.shape[0]
    order_ok = jnp.arange(block_rows)[:, None] >= jnp.arange(block_rows)[None, :]
    allowed = order_ok & (block_seg[:, None] == block_seg[None, :])
    by_head = block_cum.T
    spread = by_head[:, :, None] - by_head[:, None, :]
    decay_table = jnp.where(allowed[None], jnp.exp(jnp.where(allowed[None], spread, 0.0)), 0.0)
    scores = jnp.einsum('thd,shd->hts', query_f, key_f, precision=lax.Precision.HIGHEST)
    inside = jnp.einsum('hts,shd->thd', scores * decay_table, value_f, precision=lax.Precision.HIGHEST)
    end_seg = block_seg[-1]
    toward = jnp.where((block_seg == end_seg)[:, None], jnp.exp(block_cum[-1][None, :] - block_cum), 0.0)
    local_state = jnp.einsum('shd,she->hde', key_f * toward[:, :, None], value_f, precision=lax.Precision.HIGHEST)
    keep_factor = jnp.where(jnp.all(linked), jnp.exp(block_cum[-1] - last_cum), 0.0)
    new_state = keep_factor[:, None, None] * run_state + local_state
    return ((new_state, block_cum[-1], end_seg), earlier + inside)

def reference(queries, keys, values, log_decay, arrival_positions, prompt_lengths, norm_gain, out_weight):
    row_order = jnp.argsort(arrival_positions)
    packed_q = queries[row_order].reshape(TOKENS, HEAD_TOTAL, DH)
    packed_k = keys[row_order].reshape(TOKENS, HEAD_TOTAL, DH)
    packed_v = values[row_order].reshape(TOKENS, HEAD_TOTAL, DH)
    packed_decay = log_decay[row_order].astype(jnp.float32)
    cumulative = jnp.cumsum(packed_decay, axis=0)
    positions = jnp.arange(TOKENS, dtype=jnp.int32)
    prompt_ends = jnp.cumsum(prompt_lengths)[:-1].astype(jnp.int32)
    segment = lax.optimization_barrier(jnp.sum((positions[:, None] >= prompt_ends[None, :]).astype(jnp.int32), axis=1)).astype(jnp.int32)
    block_size = math.gcd(TOKENS, 512)
    block_count = TOKENS // block_size
    blocks = (packed_q.reshape(block_count, block_size, HEAD_TOTAL, DH), packed_k.reshape(block_count, block_size, HEAD_TOTAL, DH), packed_v.reshape(block_count, block_size, HEAD_TOTAL, DH), cumulative.reshape(block_count, block_size, HEAD_TOTAL), segment.reshape(block_count, block_size))
    start_carry = (jnp.zeros((HEAD_TOTAL, DH, DH), jnp.float32), jnp.zeros((HEAD_TOTAL,), jnp.float32), jnp.int32(-1))
    final_carry, attention = lax.scan(block_step, start_carry, blocks)
    attention = attention.reshape(TOKENS, HEAD_TOTAL, DH)
    inv_scale = lax.rsqrt(lax.optimization_barrier(jnp.mean(attention * attention, axis=-1, keepdims=True)) + 1e-06)
    normed = (attention * inv_scale * norm_gain.reshape(HEAD_TOTAL, DH)).astype(jnp.bfloat16).reshape(TOKENS, HEAD_TOTAL * DH)
    return jnp.dot(normed, out_weight, preferred_element_type=jnp.float32).astype(jnp.bfloat16)
```

```python
import functools

import jax
import jax.numpy as jnp
from jax import lax
from jax.experimental import pallas as pl
from jax.experimental.pallas import tpu as pltpu
from jax.sharding import PartitionSpec as P


def split_terms(source):
    upper_part = source.astype(jnp.bfloat16)
    lower_part = (source - upper_part.astype(jnp.float32)).astype(jnp.bfloat16)
    return (upper_part, lower_part)


def paired_einsum(form, wide_operand, narrow_operand, wide_first):
    upper_part, lower_part = split_terms(wide_operand)
    if wide_first:
        return jnp.einsum(
            form, upper_part, narrow_operand, preferred_element_type=jnp.float32
        ) + jnp.einsum(form, lower_part, narrow_operand, preferred_element_type=jnp.float32)
    return jnp.einsum(
        form, narrow_operand, upper_part, preferred_element_type=jnp.float32
    ) + jnp.einsum(form, narrow_operand, lower_part, preferred_element_type=jnp.float32)


def block_terms(run_state, last_seg, block_q, block_k, block_v, block_cum, block_seg):
    linked = block_seg == last_seg
    reach_back = jnp.where(linked[:, None], jnp.exp(block_cum), 0.0)
    earlier = paired_einsum("thd,hde->the", run_state, block_q, False) * reach_back[:, :, None]
    block_rows = block_seg.shape[0]
    order_ok = jnp.arange(block_rows)[:, None] >= jnp.arange(block_rows)[None, :]
    allowed = order_ok & (block_seg[:, None] == block_seg[None, :])
    by_head = block_cum.T
    spread = by_head[:, :, None] - by_head[:, None, :]
    decay_table = jnp.where(allowed[None], jnp.exp(jnp.where(allowed[None], spread, 0.0)), 0.0)
    scores = jnp.einsum("thd,shd->hts", block_q, block_k, preferred_element_type=jnp.float32)
    inside = paired_einsum("hts,shd->thd", scores * decay_table, block_v, True)
    end_seg = block_seg[-1]
    toward = jnp.where(
        (block_seg == end_seg)[:, None], jnp.exp(block_cum[-1][None, :] - block_cum), 0.0
    )
    local_state = paired_einsum(
        "shd,she->hde", block_k.astype(jnp.float32) * toward[:, :, None], block_v, True
    )
    keep_factor = jnp.where(jnp.all(linked), jnp.exp(block_cum[-1]), 0.0)
    new_state = keep_factor[:, None, None] * run_state + local_state
    return (earlier + inside, new_state)


def attend(own_q, own_k, own_v, cumulative, segment, run_state, last_seg):
    block_out, run_state = block_terms(
        run_state, last_seg, own_q, own_k, own_v, cumulative, segment
    )
    return (block_out, run_state)


def carried_state(factor, end_state):
    owner_count = lax.axis_size("ctx")
    my_index = lax.axis_index("ctx")
    factors, states = (
        lax.all_gather(factor[None].astype(jnp.bfloat16), "ctx", axis=0, tiled=True).astype(
            jnp.float32
        ),
        lax.all_gather(end_state[None].astype(jnp.bfloat16), "ctx", axis=0, tiled=True).astype(
            jnp.float32
        ),
    )
    index_line = jnp.arange(owner_count)
    between = (index_line[None, :] > index_line[:, None]) & (index_line[None, :] < my_index)
    chain_weights = jnp.prod(jnp.where(between[:, :, None], factors[None, :, :], 1.0), axis=1)
    chain_weights = chain_weights * (index_line < my_index)[:, None].astype(jnp.float32)
    return jnp.einsum("nh,nhde->hde", chain_weights, states, precision=lax.Precision.HIGHEST)


def exchange_form(
    queries, keys, values, log_decay, arrival_positions, prompt_lengths, norm_gain, out_weight
):
    row_count = queries.shape[0]
    heads_here = log_decay.shape[1]
    head_width = queries.shape[1] // heads_here
    owner_count = lax.axis_size("ctx")
    my_index = lax.axis_index("ctx")
    capacity = 3 * (row_count // (2 * owner_count))
    slot_total = owner_count * capacity
    every_position = lax.all_gather(arrival_positions, "ctx", axis=0, tiled=True)
    target = arrival_positions // row_count
    hit_table = (target[:, None] == jnp.arange(owner_count)[None, :]).astype(jnp.int32)
    slot_index = jnp.sum((jnp.cumsum(hit_table, axis=0) - 1) * hit_table, axis=1)
    send_slot = target * capacity + slot_index
    send_onehot = (jnp.arange(slot_total)[:, None] == send_slot[None, :]).astype(jnp.bfloat16)

    def pack_rows(source):
        packed = jnp.dot(send_onehot, source, preferred_element_type=jnp.float32).astype(
            source.dtype
        )
        return packed.reshape(owner_count, capacity, source.shape[1])

    arrived = (
        lax.all_to_all(pack_rows(queries), "ctx", split_axis=0, concat_axis=0, tiled=True),
        lax.all_to_all(pack_rows(keys), "ctx", split_axis=0, concat_axis=0, tiled=True),
        lax.all_to_all(pack_rows(values), "ctx", split_axis=0, concat_axis=0, tiled=True),
        lax.all_to_all(pack_rows(log_decay), "ctx", split_axis=0, concat_axis=0, tiled=True),
    )
    layout = every_position.reshape(owner_count, row_count)
    own_rows = layout // row_count == my_index
    rank_index = jnp.cumsum(own_rows.astype(jnp.int32), axis=1) - 1
    source_slot = (jnp.arange(owner_count)[:, None] * capacity + rank_index).reshape(-1)
    wanted = my_index * row_count + jnp.arange(row_count, dtype=jnp.int32)
    matches = every_position[None, :] == wanted[:, None]
    slot_of_row = jnp.sum(jnp.where(matches, source_slot[None, :], 0), axis=1)
    receive_onehot = (slot_of_row[:, None] == jnp.arange(slot_total)[None, :]).astype(jnp.bfloat16)

    def unpack_rows(buffer):
        flat_buffer = buffer.reshape(slot_total, buffer.shape[2])
        return jnp.dot(receive_onehot, flat_buffer, preferred_element_type=jnp.float32).astype(
            buffer.dtype
        )

    own_q = unpack_rows(arrived[0]).reshape(row_count, heads_here, head_width)
    own_k = unpack_rows(arrived[1]).reshape(row_count, heads_here, head_width)
    own_v = unpack_rows(arrived[2]).reshape(row_count, heads_here, head_width)
    cumulative = jnp.cumsum(unpack_rows(arrived[3]).astype(jnp.float32), axis=0)
    positions = my_index * row_count + jnp.arange(row_count, dtype=jnp.int32)
    prompt_ends = jnp.cumsum(prompt_lengths)[:-1]
    segment = jnp.sum((positions[:, None] >= prompt_ends[None, :]).astype(jnp.int32), axis=1)
    opens_prompt = (positions[0] == 0) | jnp.any(positions[0] == prompt_ends)
    through = jnp.logical_not(opens_prompt) & jnp.all(segment == segment[0])
    factor = jnp.where(through, jnp.exp(cumulative[-1]), 0.0)
    entry_seg = jnp.where(opens_prompt, -1, segment[0])
    empty_state = jnp.zeros((heads_here, head_width, head_width), jnp.float32)
    attention, end_state = attend(
        own_q, own_k, own_v, cumulative, segment, empty_state, jnp.int32(-1)
    )
    incoming = carried_state(factor, end_state)
    reach_back = jnp.where((segment == entry_seg)[:, None], jnp.exp(cumulative), 0.0)
    attention = (
        attention + paired_einsum("thd,hde->the", incoming, own_q, False) * reach_back[:, :, None]
    )
    inv_scale = lax.rsqrt(jnp.mean(attention * attention, axis=-1, keepdims=True) + 1e-06)
    normed = (attention * inv_scale * norm_gain.reshape(heads_here, head_width)).astype(
        jnp.bfloat16
    )
    normed = normed.reshape(row_count, heads_here * head_width)
    projected = jnp.dot(
        lax.all_gather(normed, "head", axis=1, tiled=True),
        out_weight,
        preferred_element_type=jnp.float32,
    )
    return projected.astype(jnp.bfloat16)


MESH = pl.DeviceIdType.MESH
NT = (((1,), (1,)), ((), ()))
TN = (((0,), (0,)), ((), ()))
STRIPE = 32


def dot32(left, right, dims=(((1,), (0,)), ((), ()))):
    return lax.dot_general(left, right, dims, preferred_element_type=jnp.float32)


def state_kernel(
    owners,
    rows,
    heads,
    lanes,
    slots,
    prompts,
    lengths_ref,
    pos_ref,
    decay_ref,
    gain_ref,
    q_ref,
    k_ref,
    v_ref,
    w_ref,
    out_ref,
    all_pos,
    all_decay,
    raw_in,
    ordered,
    sort_hot,
    place_hot,
    mask_bias,
    cum_col,
    cum_row,
    toward_col,
    reach_col,
    first_row,
    last_row,
    factor,
    states,
    merged,
    merged_in,
    prefix,
    normed,
    arrived,
    gathered,
    weights,
    total,
    meta_l,
    meta_s,
    meta_r,
    in_l,
    w_l,
    raw_s,
    raw_r,
    merged_s,
    merged_r,
    out_l,
    out_s,
    out_r,
    sib_s,
    sib_r,
    cross_s,
    cross_r,
    relay_s,
    relay_r,
):
    me = lax.axis_index("ctx")
    my_head = lax.axis_index("head")
    sibling = my_head + 1 - 2 * lax.rem(my_head, 2)
    cross = lax.rem(my_head + 2, 4)
    diagonal = lax.rem(sibling + 2, 4)
    tokens = owners * rows
    pairs = heads // 2
    wide = 2 * lanes
    peers = [lax.rem(me + step, owners) for step in (2, 1, 3)]
    far = jnp.where(me < 2, 2, 1)
    near = 3 - far
    edge = jnp.where(me < 2, 0, 3)
    inner = jnp.logical_or(me == 1, me == 2)
    outer = jnp.logical_not(inner)
    sources = (q_ref, k_ref, v_ref)

    def pair_block(index):
        return pl.ds(pl.multiple_of(index * wide, wide), wide)

    def lane_block(index):
        return pl.ds(pl.multiple_of(index * lanes, lanes), lanes)

    def token_block(index):
        return pl.ds(pl.multiple_of(index * rows, rows), rows)

    def in_local(a, p):
        return pltpu.make_async_copy(
            sources[a].at[:, pair_block(p)], raw_in.at[a, p], in_l.at[a, p]
        )

    def weight_load(h):
        return pltpu.make_async_copy(w_ref.at[:, h], weights.at[h], w_l.at[h])

    for p in range(pairs):
        for a in range(3):
            in_local(a, p).start()

    barrier = pltpu.get_barrier_semaphore()
    for peer in peers:
        pl.semaphore_signal(barrier, inc=1, device_id={"ctx": peer}, device_id_type=MESH)
    for peer in (sibling, cross):
        pl.semaphore_signal(barrier, inc=1, device_id={"head": peer}, device_id_type=MESH)

    def remote(source, target, send, recv, axis, device):
        return pltpu.make_async_remote_copy(
            src_ref=source,
            dst_ref=target,
            send_sem=send,
            recv_sem=recv,
            device_id={axis: device},
            device_id_type=MESH,
        )

    def pos_send(peer, source):
        return remote(
            pos_ref,
            all_pos.at[:, token_block(source)],
            meta_s.at[0, peer],
            meta_r.at[0, source],
            "ctx",
            peer,
        )

    def decay_send(peer, source):
        return remote(
            decay_ref,
            all_decay.at[:, token_block(source)],
            meta_s.at[1, peer],
            meta_r.at[1, source],
            "ctx",
            peer,
        )

    def raw_send(h, slot, peer, source):
        return remote(
            states.at[source, h],
            states.at[source, h],
            raw_s.at[slot, h],
            raw_r.at[source, h],
            "ctx",
            peer,
        )

    def merged_send(h):
        return remote(
            merged.at[h], merged_in.at[h], merged_s.at[h], merged_r.at[h], "ctx", edge
        )

    def out_send(h, owner, source):
        return remote(
            normed.at[h, owner],
            arrived.at[h, source],
            out_s.at[owner, h],
            out_r.at[source, h],
            "ctx",
            owner,
        )

    def out_local(h):
        return pltpu.make_async_copy(normed.at[h, me], arrived.at[h, me], out_l.at[h])

    def head_send(h, head_index, target, send, recv):
        piece = gathered.at[h, :, lane_block(head_index)]
        return remote(piece, piece, send.at[h], recv.at[h], "head", target)

    pos_local = pltpu.make_async_copy(pos_ref, all_pos.at[:, token_block(me)], meta_l.at[0])
    decay_local = pltpu.make_async_copy(
        decay_ref, all_decay.at[:, token_block(me)], meta_l.at[1]
    )
    pos_local.start()
    decay_local.start()
    for h in range(heads):
        weight_load(h).start()

    ends = []
    running = lengths_ref[0]
    for index in range(1, prompts):
        ends.append(running)
        running = running + lengths_ref[index]

    def segment_of(position):
        found = jnp.zeros_like(position)
        for end in ends:
            found = found + jnp.where(position >= end, 1, 0)
        return found

    own_pos = pos_ref[...].astype(jnp.float32)
    decay = decay_ref[...]
    slot_col = lax.broadcasted_iota(jnp.int32, (slots, 1), 0)
    slot_row = lax.broadcasted_iota(jnp.int32, (1, slots), 1)
    later = lax.broadcasted_iota(jnp.int32, (slots, slots), 0)
    sooner = lax.broadcasted_iota(jnp.int32, (slots, slots), 1)
    causal = later >= sooner
    lower = jnp.where(causal, 1.0, 0.0).astype(jnp.bfloat16)
    for o in range(owners):
        inside = (own_pos >= o * rows) & (own_pos < (o + 1) * rows)
        first = jnp.min(jnp.where(inside, own_pos, 1.0 * tokens), axis=1, keepdims=True)
        last = jnp.max(jnp.where(inside, own_pos, -1.0), axis=1, keepdims=True)
        first_at = first.astype(jnp.int32)
        last_at = last.astype(jnp.int32)
        here_col = first_at + slot_col
        here_row = first_at + slot_row
        wanted = jnp.where(here_col <= last_at, here_col, -1).astype(jnp.float32)
        hits = jnp.where(own_pos == wanted, 1.0, 0.0).astype(jnp.bfloat16)
        sort_hot[pl.ds(o * slots, slots), :] = hits
        decay_rows = dot32(decay, hits, NT).astype(jnp.bfloat16)
        decay_cols = dot32(hits, decay, NT).astype(jnp.bfloat16)
        row_sums = dot32(decay_rows, lower, NT)
        col_sums = dot32(lower, decay_cols)
        cum_row[o] = row_sums
        seg_col = segment_of(here_col)
        seg_row = segment_of(here_row)
        seg_first = segment_of(first_at)
        seg_last = segment_of(last_at)
        mask_bias[o] = jnp.where(causal & (seg_col == seg_row), 0.0, -1e30)
        toward = jnp.where(
            seg_col == seg_last, jnp.exp(col_sums[slots - 1 :, :] - col_sums), 0.0
        )
        reach = jnp.where(seg_col == seg_first, jnp.exp(col_sums), 0.0)
        for p in range(pairs):
            cum_col[p, o] = col_sums[:, 2 * p : 2 * p + 2]
            toward_col[p, o] = toward[:, 2 * p : 2 * p + 2]
            reach_col[p, o] = reach[:, 2 * p : 2 * p + 2]

    pl.semaphore_wait(barrier, owners + 1)
    for peer in peers:
        pos_send(peer, me).start()
        decay_send(peer, me).start()

    half = owners * slots // 2

    def make_states(p, carry):
        for a in range(3):
            in_local(a, p).wait()
            for part in range(2):
                block = pl.ds(part * half, half)
                ordered[a, p, block, :] = dot32(sort_hot[block, :], raw_in[a, p]).astype(
                    jnp.bfloat16
                )
        for j in range(2):
            h = 2 * p + j
            for o in range(owners):
                run = pl.ds(o * slots, slots)
                side = slice(j * lanes, (j + 1) * lanes)
                key = ordered[1, p, run, side]
                value = ordered[2, p, run, side]
                weighted = key.astype(jnp.float32) * toward_col[p, o][:, j : j + 1]
                states[me, h, o] = dot32(weighted.astype(jnp.bfloat16), value, TN).astype(
                    jnp.bfloat16
                )
            raw_send(h, 0, far, me).start()

            @pl.when(outer)
            def _():
                raw_send(h, 1, near, me).start()

        return carry

    lax.fori_loop(0, pairs, make_states, 0)

    pos_local.wait()
    decay_local.wait()
    for peer in peers:
        pos_send(me, peer).wait_recv()
        decay_send(me, peer).wait_recv()

    group_iota = lax.broadcasted_iota(jnp.int32, (8, rows), 0).astype(jnp.float32) * rows
    for d in range(owners):
        held = all_pos[:, d * rows : (d + 1) * rows].astype(jnp.float32)
        inside = (held >= group_iota) & (held < group_iota + rows)
        first = jnp.min(jnp.where(inside, held, 1.0 * tokens), axis=1, keepdims=True)
        last = jnp.max(jnp.where(inside, held, -1.0), axis=1, keepdims=True)
        first_row[d * 8 : d * 8 + 8, :] = jnp.broadcast_to(first, (8, lanes))
        last_row[d * 8 : d * 8 + 8, :] = jnp.broadcast_to(last, (8, lanes))

    every_pos = all_pos[...].astype(jnp.float32)
    every_decay = all_decay[...]
    last_all = last_row[...][:, :1]
    seg_all = segment_of(last_all.astype(jnp.int32))
    holder = lax.broadcasted_iota(jnp.int32, (8 * owners, 1), 0) // 8
    for t in range(2 * owners):
        device = me if t < owners else edge
        start = first_row[pl.ds(device * 8 + t % owners, 1), :][:, :1]
        between = (every_pos > last_all) & (every_pos < start)
        sums = dot32(jnp.where(between, 1.0, 0.0).astype(jnp.bfloat16), every_decay, NT)
        linked = (last_all < start) & (seg_all == segment_of(start.astype(jnp.int32)))
        if t >= owners:
            linked = linked & (holder != edge)
        scale = jnp.where(linked, jnp.exp(sums), 0.0)
        for h in range(heads):
            factor[h, t] = jnp.broadcast_to(scale[:, h : h + 1], (8 * owners, lanes))

    line = lax.broadcasted_iota(jnp.int32, (1, owners * slots), 1).astype(jnp.float32)
    source_pos = jnp.full((1, owners * slots), -1.0, jnp.float32)
    for d in range(owners):
        first = first_row[pl.ds(d * 8 + me, 1), :][:, :1]
        last = last_row[pl.ds(d * 8 + me, 1), :][:, :1]
        found = first + (line - 1.0 * d * slots)
        fine = (line >= d * slots) & (line < (d + 1) * slots) & (found <= last)
        source_pos = jnp.where(fine, found, source_pos)
    target_pos = (me * rows + lax.broadcasted_iota(jnp.int32, (rows, 1), 0)).astype(jnp.float32)
    place_hot[...] = jnp.where(target_pos == source_pos, 1.0, 0.0).astype(jnp.bfloat16)
    total[...] = jnp.zeros_like(total)

    def stripe(index):
        return pl.ds(pl.multiple_of(index * STRIPE, STRIPE), STRIPE)

    def merge_inner(h):
        def body(index, carry):
            block = stripe(index)
            sums = [None] * (2 * owners)
            for d in range(owners):
                for past in range(owners):
                    tile = states[d, h, past, block, :].astype(jnp.float32)
                    for t in range(2 * owners):
                        if past <= t % owners:
                            term = tile * factor[h, t, pl.ds(d * 8 + past, 1), :]
                            sums[t] = term if sums[t] is None else sums[t] + term
            for o in range(owners):
                prefix[o, block, :] = sums[o].astype(jnp.bfloat16)
                merged[h, o, block, :] = sums[owners + o].astype(jnp.bfloat16)
            return carry

        lax.fori_loop(0, lanes // STRIPE, body, 0)

    def merge_outer(h):
        def body(index, carry):
            block = stripe(index)
            for o in range(owners):
                summed = merged_in[h, o, block, :].astype(jnp.float32)
                for past in range(o):
                    tile = states[me, h, past, block, :].astype(jnp.float32)
                    summed = summed + tile * factor[h, o, pl.ds(me * 8 + past, 1), :]
                prefix[o, block, :] = summed.astype(jnp.bfloat16)
            return carry

        lax.fori_loop(0, lanes // STRIPE, body, 0)

    def attend_pair(p, carry):
        for j in range(2):
            h = 2 * p + j

            @pl.when(inner)
            def _():
                for peer in peers:
                    raw_send(h, 0, me, peer).wait_recv()
                merge_inner(h)
                merged_send(h).start()

            @pl.when(outer)
            def _():
                merged_send(h).wait_recv()
                merge_outer(h)

            gain = gain_ref[pl.ds(h, 1), :]
            for o in range(owners):
                run = pl.ds(o * slots, slots)
                side = slice(j * lanes, (j + 1) * lanes)
                query = ordered[0, p, run, side]
                key = ordered[1, p, run, side]
                value = ordered[2, p, run, side]
                col = cum_col[p, o][:, j : j + 1]
                row = cum_row[o, pl.ds(h, 1), :]
                table = jnp.exp(col - row + mask_bias[o])
                scores = (dot32(query, key, NT) * table).astype(jnp.bfloat16)
                result = dot32(scores, value)
                result = result + dot32(query, prefix[o]) * reach_col[p, o][:, j : j + 1]
                scale = lax.rsqrt(jnp.mean(result * result, axis=-1, keepdims=True) + 1e-06)
                normed[h, o] = (result * scale * gain).astype(jnp.bfloat16)
            for peer in peers:
                out_send(h, peer, me).start()
            out_local(h).start()
        return carry

    lax.fori_loop(0, pairs, attend_pair, 0)

    def place(h):
        out_local(h).wait()
        for peer in peers:
            out_send(h, me, peer).wait_recv()
        incoming = arrived[h].reshape(owners * slots, lanes)
        gathered[h, :, lane_block(my_head)] = dot32(place_hot[...], incoming).astype(
            jnp.bfloat16
        )
        head_send(h, my_head, cross, cross_s, cross_r).start()
        head_send(h, my_head, sibling, sib_s, sib_r).start()

    def relay(h):
        head_send(h, cross, cross, cross_s, cross_r).wait_recv()
        head_send(h, cross, sibling, relay_s, relay_r).start()

    width = out_ref.shape[1]
    tile = 256

    def project(h, final):
        head_send(h, sibling, sibling, sib_s, sib_r).wait_recv()
        head_send(h, diagonal, sibling, relay_s, relay_r).wait_recv()

        def columns_of(index, carry):
            columns = pl.ds(pl.multiple_of(index * tile, tile), tile)
            right = weights[h, :, :, columns].reshape(4 * lanes, tile)
            summed = total[:, columns] + dot32(gathered[h], right)
            if final:
                out_ref[:, columns] = summed.astype(out_ref.dtype)
            else:
                total[:, columns] = summed
            return carry

        lax.fori_loop(0, width // tile, columns_of, 0)

    for h in range(heads):
        weight_load(h).wait()

    def finish_pair(p, carry):
        @pl.when(p > 0)
        def _():
            relay(2 * p - 1)

        place(2 * p)

        @pl.when(p > 0)
        def _():
            project(2 * p - 1, False)

        relay(2 * p)
        place(2 * p + 1)
        project(2 * p, False)
        return carry

    lax.fori_loop(0, pairs, finish_pair, 0)
    relay(heads - 1)
    project(heads - 1, True)

    for peer in peers:
        pos_send(peer, me).wait_send()
        decay_send(peer, me).wait_send()

    def drain(h, carry):
        raw_send(h, 0, far, me).wait_send()

        @pl.when(outer)
        def _():
            raw_send(h, 1, near, me).wait_send()

        @pl.when(inner)
        def _():
            merged_send(h).wait_send()

        for peer in peers:
            out_send(h, peer, me).wait_send()
        head_send(h, my_head, cross, cross_s, cross_r).wait_send()
        head_send(h, my_head, sibling, sib_s, sib_r).wait_send()
        head_send(h, cross, sibling, relay_s, relay_r).wait_send()
        return carry

    lax.fori_loop(0, heads, drain, 0)


def fused_form(
    queries, keys, values, log_decay, arrival_positions, prompt_lengths, norm_gain, out_weight
):
    rows = queries.shape[0]
    heads = log_decay.shape[1]
    lanes = queries.shape[1] // heads
    owners = lax.axis_size("ctx")
    columns = lax.axis_size("head")
    tokens = owners * rows
    slots = 3 * (rows // (2 * owners))
    pairs = heads // 2
    wide = 2 * lanes
    padded = owners * slots
    features, width = out_weight.shape
    gain = norm_gain.reshape(heads, lanes)
    stacked = out_weight.reshape(columns, heads, lanes, width)
    vmem = pl.BlockSpec(memory_space=pltpu.VMEM)
    anywhere = pl.BlockSpec(memory_space=pl.ANY)
    dma = pltpu.SemaphoreType.DMA
    bf16, f32 = jnp.bfloat16, jnp.float32
    return pl.pallas_call(
        functools.partial(
            state_kernel, owners, rows, heads, lanes, slots, prompt_lengths.shape[0]
        ),
        out_shape=jax.ShapeDtypeStruct((rows, width), bf16),
        in_specs=[
            pl.BlockSpec(memory_space=pltpu.SMEM),
            vmem,
            vmem,
            vmem,
            anywhere,
            anywhere,
            anywhere,
            anywhere,
        ],
        out_specs=vmem,
        scratch_shapes=[
            pltpu.VMEM((1, tokens), jnp.int32),
            pltpu.VMEM((heads, tokens), bf16),
            pltpu.VMEM((3, pairs, rows, wide), bf16),
            pltpu.VMEM((3, pairs, padded, wide), bf16),
            pltpu.VMEM((padded, rows), bf16),
            pltpu.VMEM((rows, padded), bf16),
            pltpu.VMEM((owners, slots, slots), f32),
            pltpu.VMEM((pairs, owners, slots, 2), f32),
            pltpu.VMEM((owners, heads, slots), f32),
            pltpu.VMEM((pairs, owners, slots, 2), f32),
            pltpu.VMEM((pairs, owners, slots, 2), f32),
            pltpu.VMEM((8 * owners, lanes), f32),
            pltpu.VMEM((8 * owners, lanes), f32),
            pltpu.VMEM((heads, 2 * owners, 8 * owners, lanes), f32),
            pltpu.VMEM((owners, heads, owners, lanes, lanes), bf16),
            pltpu.VMEM((heads, owners, lanes, lanes), bf16),
            pltpu.VMEM((heads, owners, lanes, lanes), bf16),
            pltpu.VMEM((owners, lanes, lanes), bf16),
            pltpu.VMEM((heads, owners, slots, lanes), bf16),
            pltpu.VMEM((heads, owners, slots, lanes), bf16),
            pltpu.VMEM((heads, rows, columns * lanes), bf16),
            pltpu.VMEM((heads, columns, lanes, width), bf16),
            pltpu.VMEM((rows, width), f32),
            dma((2,)),
            dma((2, owners)),
            dma((2, owners)),
            dma((3, pairs)),
            dma((heads,)),
            dma((2, heads)),
            dma((owners, heads)),
            dma((heads,)),
            dma((heads,)),
            dma((heads,)),
            dma((owners, heads)),
            dma((owners, heads)),
            dma((heads,)),
            dma((heads,)),
            dma((heads,)),
            dma((heads,)),
            dma((heads,)),
            dma((heads,)),
        ],
        compiler_params=pltpu.CompilerParams(
            collective_id=0, has_side_effects=True, vmem_limit_bytes=58 * 1024 * 1024
        ),
    )(
        prompt_lengths,
        arrival_positions.reshape(1, rows),
        log_decay.T,
        gain,
        queries,
        keys,
        values,
        stacked,
    )


def local(*arguments):
    queries, log_decay = arguments[0], arguments[3]
    fits = (
        log_decay.shape[1] == 8
        and lax.axis_size("ctx") == 4
        and lax.axis_size("head") == 4
        and queries.shape[0] == 512
        and queries.shape[1] == 128 * log_decay.shape[1]
    )
    return (fused_form if fits else exchange_form)(*arguments)


def solution(mesh):
    return jax.shard_map(
        local,
        mesh=mesh,
        in_specs=(
            P(("groups", "ctx"), "head"),
            P(("groups", "ctx"), "head"),
            P(("groups", "ctx"), "head"),
            P(("groups", "ctx"), "head"),
            P(("groups", "ctx")),
            P("groups"),
            P("head"),
            P(None, "head"),
        ),
        out_specs=P(("groups", "ctx"), "head"),
        check_vma=False,
    )
```

```python
import functools

import jax
import jax.numpy as jnp
from jax import lax
from jax.experimental import pallas as pl
from jax.experimental.pallas import tpu as pltpu
from jax.sharding import PartitionSpec as P


def split_terms(source):
    upper_part = source.astype(jnp.bfloat16)
    lower_part = (source - upper_part.astype(jnp.float32)).astype(jnp.bfloat16)
    return (upper_part, lower_part)


def paired_einsum(form, wide_operand, narrow_operand, wide_first):
    upper_part, lower_part = split_terms(wide_operand)
    if wide_first:
        return jnp.einsum(
            form, upper_part, narrow_operand, preferred_element_type=jnp.float32
        ) + jnp.einsum(form, lower_part, narrow_operand, preferred_element_type=jnp.float32)
    return jnp.einsum(
        form, narrow_operand, upper_part, preferred_element_type=jnp.float32
    ) + jnp.einsum(form, narrow_operand, lower_part, preferred_element_type=jnp.float32)


def block_terms(run_state, last_seg, block_q, block_k, block_v, block_cum, block_seg):
    linked = block_seg == last_seg
    reach_back = jnp.where(linked[:, None], jnp.exp(block_cum), 0.0)
    earlier = paired_einsum("thd,hde->the", run_state, block_q, False) * reach_back[:, :, None]
    block_rows = block_seg.shape[0]
    order_ok = jnp.arange(block_rows)[:, None] >= jnp.arange(block_rows)[None, :]
    allowed = order_ok & (block_seg[:, None] == block_seg[None, :])
    by_head = block_cum.T
    spread = by_head[:, :, None] - by_head[:, None, :]
    decay_table = jnp.where(allowed[None], jnp.exp(jnp.where(allowed[None], spread, 0.0)), 0.0)
    scores = jnp.einsum("thd,shd->hts", block_q, block_k, preferred_element_type=jnp.float32)
    inside = paired_einsum("hts,shd->thd", scores * decay_table, block_v, True)
    end_seg = block_seg[-1]
    toward = jnp.where(
        (block_seg == end_seg)[:, None], jnp.exp(block_cum[-1][None, :] - block_cum), 0.0
    )
    local_state = paired_einsum(
        "shd,she->hde", block_k.astype(jnp.float32) * toward[:, :, None], block_v, True
    )
    keep_factor = jnp.where(jnp.all(linked), jnp.exp(block_cum[-1]), 0.0)
    new_state = keep_factor[:, None, None] * run_state + local_state
    return (earlier + inside, new_state)


def attend(own_q, own_k, own_v, cumulative, segment, run_state, last_seg):
    block_out, run_state = block_terms(
        run_state, last_seg, own_q, own_k, own_v, cumulative, segment
    )
    return (block_out, run_state)


def carried_state(factor, end_state):
    owner_count = lax.axis_size("ctx")
    my_index = lax.axis_index("ctx")
    factors, states = (
        lax.all_gather(factor[None].astype(jnp.bfloat16), "ctx", axis=0, tiled=True).astype(
            jnp.float32
        ),
        lax.all_gather(end_state[None].astype(jnp.bfloat16), "ctx", axis=0, tiled=True).astype(
            jnp.float32
        ),
    )
    index_line = jnp.arange(owner_count)
    between = (index_line[None, :] > index_line[:, None]) & (index_line[None, :] < my_index)
    chain_weights = jnp.prod(jnp.where(between[:, :, None], factors[None, :, :], 1.0), axis=1)
    chain_weights = chain_weights * (index_line < my_index)[:, None].astype(jnp.float32)
    return jnp.einsum("nh,nhde->hde", chain_weights, states, precision=lax.Precision.HIGHEST)


def exchange_form(
    queries, keys, values, log_decay, arrival_positions, prompt_lengths, norm_gain, out_weight
):
    row_count = queries.shape[0]
    heads_here = log_decay.shape[1]
    head_width = queries.shape[1] // heads_here
    owner_count = lax.axis_size("ctx")
    my_index = lax.axis_index("ctx")
    capacity = 3 * (row_count // (2 * owner_count))
    slot_total = owner_count * capacity
    every_position = lax.all_gather(arrival_positions, "ctx", axis=0, tiled=True)
    target = arrival_positions // row_count
    hit_table = (target[:, None] == jnp.arange(owner_count)[None, :]).astype(jnp.int32)
    slot_index = jnp.sum((jnp.cumsum(hit_table, axis=0) - 1) * hit_table, axis=1)
    send_slot = target * capacity + slot_index
    send_onehot = (jnp.arange(slot_total)[:, None] == send_slot[None, :]).astype(jnp.bfloat16)

    def pack_rows(source):
        packed = jnp.dot(send_onehot, source, preferred_element_type=jnp.float32).astype(
            source.dtype
        )
        return packed.reshape(owner_count, capacity, source.shape[1])

    arrived = (
        lax.all_to_all(pack_rows(queries), "ctx", split_axis=0, concat_axis=0, tiled=True),
        lax.all_to_all(pack_rows(keys), "ctx", split_axis=0, concat_axis=0, tiled=True),
        lax.all_to_all(pack_rows(values), "ctx", split_axis=0, concat_axis=0, tiled=True),
        lax.all_to_all(pack_rows(log_decay), "ctx", split_axis=0, concat_axis=0, tiled=True),
    )
    layout = every_position.reshape(owner_count, row_count)
    own_rows = layout // row_count == my_index
    rank_index = jnp.cumsum(own_rows.astype(jnp.int32), axis=1) - 1
    source_slot = (jnp.arange(owner_count)[:, None] * capacity + rank_index).reshape(-1)
    wanted = my_index * row_count + jnp.arange(row_count, dtype=jnp.int32)
    matches = every_position[None, :] == wanted[:, None]
    slot_of_row = jnp.sum(jnp.where(matches, source_slot[None, :], 0), axis=1)
    receive_onehot = (slot_of_row[:, None] == jnp.arange(slot_total)[None, :]).astype(jnp.bfloat16)

    def unpack_rows(buffer):
        flat_buffer = buffer.reshape(slot_total, buffer.shape[2])
        return jnp.dot(receive_onehot, flat_buffer, preferred_element_type=jnp.float32).astype(
            buffer.dtype
        )

    own_q = unpack_rows(arrived[0]).reshape(row_count, heads_here, head_width)
    own_k = unpack_rows(arrived[1]).reshape(row_count, heads_here, head_width)
    own_v = unpack_rows(arrived[2]).reshape(row_count, heads_here, head_width)
    cumulative = jnp.cumsum(unpack_rows(arrived[3]).astype(jnp.float32), axis=0)
    positions = my_index * row_count + jnp.arange(row_count, dtype=jnp.int32)
    prompt_ends = jnp.cumsum(prompt_lengths)[:-1]
    segment = jnp.sum((positions[:, None] >= prompt_ends[None, :]).astype(jnp.int32), axis=1)
    opens_prompt = (positions[0] == 0) | jnp.any(positions[0] == prompt_ends)
    through = jnp.logical_not(opens_prompt) & jnp.all(segment == segment[0])
    factor = jnp.where(through, jnp.exp(cumulative[-1]), 0.0)
    entry_seg = jnp.where(opens_prompt, -1, segment[0])
    empty_state = jnp.zeros((heads_here, head_width, head_width), jnp.float32)
    attention, end_state = attend(
        own_q, own_k, own_v, cumulative, segment, empty_state, jnp.int32(-1)
    )
    incoming = carried_state(factor, end_state)
    reach_back = jnp.where((segment == entry_seg)[:, None], jnp.exp(cumulative), 0.0)
    attention = (
        attention + paired_einsum("thd,hde->the", incoming, own_q, False) * reach_back[:, :, None]
    )
    inv_scale = lax.rsqrt(jnp.mean(attention * attention, axis=-1, keepdims=True) + 1e-06)
    normed = (attention * inv_scale * norm_gain.reshape(heads_here, head_width)).astype(
        jnp.bfloat16
    )
    normed = normed.reshape(row_count, heads_here * head_width)
    projected = jnp.dot(
        lax.all_gather(normed, "head", axis=1, tiled=True),
        out_weight,
        preferred_element_type=jnp.float32,
    )
    return projected.astype(jnp.bfloat16)


MESH = pl.DeviceIdType.MESH
NT = (((1,), (1,)), ((), ()))
TN = (((0,), (0,)), ((), ()))
STRIPE = 32


def dot32(left, right, dims=(((1,), (0,)), ((), ()))):
    return lax.dot_general(left, right, dims, preferred_element_type=jnp.float32)


def state_kernel(
    owners,
    rows,
    heads,
    lanes,
    slots,
    prompts,
    lengths_ref,
    pos_ref,
    decay_ref,
    gain_ref,
    q_ref,
    k_ref,
    v_ref,
    w_ref,
    out_ref,
    all_pos,
    all_decay,
    raw_in,
    ordered,
    sort_hot,
    place_hot,
    mask_bias,
    cum_col,
    cum_row,
    toward_col,
    reach_col,
    first_row,
    last_row,
    factor,
    states,
    merged,
    merged_in,
    prefix,
    normed,
    arrived,
    gathered,
    weights,
    total,
    meta_l,
    meta_s,
    meta_r,
    in_l,
    w_l,
    raw_s,
    raw_r,
    merged_s,
    merged_r,
    out_l,
    out_s,
    out_r,
    sib_s,
    sib_r,
    cross_s,
    cross_r,
    relay_s,
    relay_r,
):
    me = lax.axis_index("ctx")
    my_head = lax.axis_index("head")
    sibling = my_head + 1 - 2 * lax.rem(my_head, 2)
    cross = lax.rem(my_head + 2, 4)
    diagonal = lax.rem(sibling + 2, 4)
    tokens = owners * rows
    pairs = heads // 2
    wide = 2 * lanes
    peers = [lax.rem(me + step, owners) for step in (2, 1, 3)]
    far = jnp.where(me < 2, 2, 1)
    near = 3 - far
    edge = jnp.where(me < 2, 0, 3)
    inner = jnp.logical_or(me == 1, me == 2)
    outer = jnp.logical_not(inner)
    sources = (q_ref, k_ref, v_ref)

    def pair_block(index):
        return pl.ds(pl.multiple_of(index * wide, wide), wide)

    def lane_block(index):
        return pl.ds(pl.multiple_of(index * lanes, lanes), lanes)

    def token_block(index):
        return pl.ds(pl.multiple_of(index * rows, rows), rows)

    def in_local(a, p):
        return pltpu.make_async_copy(
            sources[a].at[:, pair_block(p)], raw_in.at[a, p], in_l.at[a, p]
        )

    def weight_load(h):
        return pltpu.make_async_copy(w_ref.at[:, h], weights.at[h], w_l.at[h])

    for p in range(pairs):
        for a in (1, 2):
            in_local(a, p).start()
    for p in range(pairs):
        in_local(0, p).start()

    barrier = pltpu.get_barrier_semaphore()
    for peer in peers:
        pl.semaphore_signal(barrier, inc=1, device_id={"ctx": peer}, device_id_type=MESH)
    for peer in (sibling, cross):
        pl.semaphore_signal(barrier, inc=1, device_id={"head": peer}, device_id_type=MESH)

    def remote(source, target, send, recv, axis, device):
        return pltpu.make_async_remote_copy(
            src_ref=source,
            dst_ref=target,
            send_sem=send,
            recv_sem=recv,
            device_id={axis: device},
            device_id_type=MESH,
        )

    def pos_send(peer, source):
        return remote(
            pos_ref,
            all_pos.at[:, token_block(source)],
            meta_s.at[0, peer],
            meta_r.at[0, source],
            "ctx",
            peer,
        )

    def decay_send(peer, source):
        return remote(
            decay_ref,
            all_decay.at[:, token_block(source)],
            meta_s.at[1, peer],
            meta_r.at[1, source],
            "ctx",
            peer,
        )

    def raw_send(h, slot, peer, source):
        return remote(
            states.at[source, h],
            states.at[source, h],
            raw_s.at[slot, h],
            raw_r.at[source, h],
            "ctx",
            peer,
        )

    def merged_send(h):
        return remote(
            merged.at[h], merged_in.at[h], merged_s.at[h], merged_r.at[h], "ctx", edge
        )

    def out_send(h, owner, source):
        return remote(
            normed.at[h, owner],
            arrived.at[h, source],
            out_s.at[owner, h],
            out_r.at[source, h],
            "ctx",
            owner,
        )

    def out_local(h):
        return pltpu.make_async_copy(normed.at[h, me], arrived.at[h, me], out_l.at[h])

    def head_send(h, head_index, target, send, recv):
        piece = gathered.at[h, :, lane_block(head_index)]
        return remote(piece, piece, send.at[h], recv.at[h], "head", target)

    pos_local = pltpu.make_async_copy(pos_ref, all_pos.at[:, token_block(me)], meta_l.at[0])
    decay_local = pltpu.make_async_copy(
        decay_ref, all_decay.at[:, token_block(me)], meta_l.at[1]
    )
    pos_local.start()
    decay_local.start()
    for h in range(heads):
        weight_load(h).start()

    ends = []
    running = lengths_ref[0]
    for index in range(1, prompts):
        ends.append(running)
        running = running + lengths_ref[index]

    def segment_of(position):
        found = jnp.zeros_like(position)
        for end in ends:
            found = found + jnp.where(position >= end, 1, 0)
        return found

    own_pos = pos_ref[...].astype(jnp.float32)
    decay = decay_ref[...]
    slot_col = lax.broadcasted_iota(jnp.int32, (slots, 1), 0)
    slot_row = lax.broadcasted_iota(jnp.int32, (1, slots), 1)
    later = lax.broadcasted_iota(jnp.int32, (slots, slots), 0)
    sooner = lax.broadcasted_iota(jnp.int32, (slots, slots), 1)
    causal = later >= sooner
    lower = jnp.where(causal, 1.0, 0.0).astype(jnp.bfloat16)
    bounds = []
    for o in range(owners):
        inside = (own_pos >= o * rows) & (own_pos < (o + 1) * rows)
        first = jnp.min(jnp.where(inside, own_pos, 1.0 * tokens), axis=1, keepdims=True)
        last = jnp.max(jnp.where(inside, own_pos, -1.0), axis=1, keepdims=True)
        first_at = first.astype(jnp.int32)
        last_at = last.astype(jnp.int32)
        bounds.append((first_at, last_at))
        here_col = first_at + slot_col
        wanted = jnp.where(here_col <= last_at, here_col, -1).astype(jnp.float32)
        hits = jnp.where(own_pos == wanted, 1.0, 0.0).astype(jnp.bfloat16)
        sort_hot[pl.ds(o * slots, slots), :] = hits
        decay_cols = dot32(hits, decay, NT).astype(jnp.bfloat16)
        col_sums = dot32(lower, decay_cols)
        toward = jnp.where(
            segment_of(here_col) == segment_of(last_at),
            jnp.exp(col_sums[slots - 1 :, :] - col_sums),
            0.0,
        )
        for p in range(pairs):
            cum_col[p, o] = col_sums[:, 2 * p : 2 * p + 2]
            toward_col[p, o] = toward[:, 2 * p : 2 * p + 2]

    pl.semaphore_wait(barrier, owners + 1)
    for peer in peers:
        pos_send(peer, me).start()
        decay_send(peer, me).start()

    half = owners * slots // 2

    def sort_rows(a, p):
        in_local(a, p).wait()
        for part in range(2):
            block = pl.ds(part * half, half)
            ordered[a, p, block, :] = dot32(sort_hot[block, :], raw_in[a, p]).astype(
                jnp.bfloat16
            )

    def make_states(p, carry):
        sort_rows(1, p)
        sort_rows(2, p)
        for j in range(2):
            h = 2 * p + j
            for o in range(owners):
                run = pl.ds(o * slots, slots)
                side = slice(j * lanes, (j + 1) * lanes)
                key = ordered[1, p, run, side]
                value = ordered[2, p, run, side]
                weighted = key.astype(jnp.float32) * toward_col[p, o][:, j : j + 1]
                states[me, h, o] = dot32(weighted.astype(jnp.bfloat16), value, TN).astype(
                    jnp.bfloat16
                )
            raw_send(h, 0, far, me).start()

            @pl.when(outer)
            def _():
                raw_send(h, 1, near, me).start()

        return carry

    lax.fori_loop(0, pairs, make_states, 0)

    for o in range(owners):
        first_at, last_at = bounds[o]
        hits = sort_hot[pl.ds(o * slots, slots), :]
        decay_rows = dot32(decay, hits, NT).astype(jnp.bfloat16)
        cum_row[o] = dot32(decay_rows, lower, NT)
        seg_col = segment_of(first_at + slot_col)
        seg_row = segment_of(first_at + slot_row)
        seg_first = segment_of(first_at)
        mask_bias[o] = jnp.where(causal & (seg_col == seg_row), 0.0, -1e30)
        for p in range(pairs):
            reach_col[p, o] = jnp.where(seg_col == seg_first, jnp.exp(cum_col[p, o]), 0.0)

    def sort_queries(p, carry):
        sort_rows(0, p)
        return carry

    lax.fori_loop(0, pairs, sort_queries, 0)

    pos_local.wait()
    decay_local.wait()
    for peer in peers:
        pos_send(me, peer).wait_recv()
        decay_send(me, peer).wait_recv()

    group_iota = lax.broadcasted_iota(jnp.int32, (8, rows), 0).astype(jnp.float32) * rows
    for d in range(owners):
        held = all_pos[:, d * rows : (d + 1) * rows].astype(jnp.float32)
        inside = (held >= group_iota) & (held < group_iota + rows)
        first = jnp.min(jnp.where(inside, held, 1.0 * tokens), axis=1, keepdims=True)
        last = jnp.max(jnp.where(inside, held, -1.0), axis=1, keepdims=True)
        first_row[d * 8 : d * 8 + 8, :] = jnp.broadcast_to(first, (8, lanes))
        last_row[d * 8 : d * 8 + 8, :] = jnp.broadcast_to(last, (8, lanes))

    every_pos = all_pos[...].astype(jnp.float32)
    every_decay = all_decay[...]
    last_all = last_row[...][:, :1]
    seg_all = segment_of(last_all.astype(jnp.int32))
    holder = lax.broadcasted_iota(jnp.int32, (8 * owners, 1), 0) // 8
    for t in range(2 * owners):
        device = me if t < owners else edge
        start = first_row[pl.ds(device * 8 + t % owners, 1), :][:, :1]
        between = (every_pos > last_all) & (every_pos < start)
        sums = dot32(jnp.where(between, 1.0, 0.0).astype(jnp.bfloat16), every_decay, NT)
        linked = (last_all < start) & (seg_all == segment_of(start.astype(jnp.int32)))
        if t >= owners:
            linked = linked & (holder != edge)
        scale = jnp.where(linked, jnp.exp(sums), 0.0)
        for h in range(heads):
            factor[h, t] = jnp.broadcast_to(scale[:, h : h + 1], (8 * owners, lanes))

    line = lax.broadcasted_iota(jnp.int32, (1, owners * slots), 1).astype(jnp.float32)
    source_pos = jnp.full((1, owners * slots), -1.0, jnp.float32)
    for d in range(owners):
        first = first_row[pl.ds(d * 8 + me, 1), :][:, :1]
        last = last_row[pl.ds(d * 8 + me, 1), :][:, :1]
        found = first + (line - 1.0 * d * slots)
        fine = (line >= d * slots) & (line < (d + 1) * slots) & (found <= last)
        source_pos = jnp.where(fine, found, source_pos)
    target_pos = (me * rows + lax.broadcasted_iota(jnp.int32, (rows, 1), 0)).astype(jnp.float32)
    place_hot[...] = jnp.where(target_pos == source_pos, 1.0, 0.0).astype(jnp.bfloat16)
    total[...] = jnp.zeros_like(total)

    def stripe(index):
        return pl.ds(pl.multiple_of(index * STRIPE, STRIPE), STRIPE)

    def merge_inner(h):
        def body(index, carry):
            block = stripe(index)
            sums = [None] * (2 * owners)
            for d in range(owners):
                for past in range(owners):
                    tile = states[d, h, past, block, :].astype(jnp.float32)
                    for t in range(2 * owners):
                        if past <= t % owners:
                            term = tile * factor[h, t, pl.ds(d * 8 + past, 1), :]
                            sums[t] = term if sums[t] is None else sums[t] + term
            for o in range(owners):
                prefix[o, block, :] = sums[o].astype(jnp.bfloat16)
                merged[h, o, block, :] = sums[owners + o].astype(jnp.bfloat16)
            return carry

        lax.fori_loop(0, lanes // STRIPE, body, 0)

    def merge_outer(h):
        def body(index, carry):
            block = stripe(index)
            for o in range(owners):
                summed = merged_in[h, o, block, :].astype(jnp.float32)
                for past in range(o):
                    tile = states[me, h, past, block, :].astype(jnp.float32)
                    summed = summed + tile * factor[h, o, pl.ds(me * 8 + past, 1), :]
                prefix[o, block, :] = summed.astype(jnp.bfloat16)
            return carry

        lax.fori_loop(0, lanes // STRIPE, body, 0)

    def attend_pair(p, carry):
        for j in range(2):
            h = 2 * p + j

            @pl.when(inner)
            def _():
                for peer in peers:
                    raw_send(h, 0, me, peer).wait_recv()
                merge_inner(h)
                merged_send(h).start()

            @pl.when(outer)
            def _():
                merged_send(h).wait_recv()
                merge_outer(h)

            gain = gain_ref[pl.ds(h, 1), :]
            for o in range(owners):
                run = pl.ds(o * slots, slots)
                side = slice(j * lanes, (j + 1) * lanes)
                query = ordered[0, p, run, side]
                key = ordered[1, p, run, side]
                value = ordered[2, p, run, side]
                col = cum_col[p, o][:, j : j + 1]
                row = cum_row[o, pl.ds(h, 1), :]
                table = jnp.exp(col - row + mask_bias[o])
                scores = (dot32(query, key, NT) * table).astype(jnp.bfloat16)
                result = dot32(scores, value)
                result = result + dot32(query, prefix[o]) * reach_col[p, o][:, j : j + 1]
                scale = lax.rsqrt(jnp.mean(result * result, axis=-1, keepdims=True) + 1e-06)
                normed[h, o] = (result * scale * gain).astype(jnp.bfloat16)
            for peer in peers:
                out_send(h, peer, me).start()
            out_local(h).start()
        return carry

    lax.fori_loop(0, pairs, attend_pair, 0)

    def place(h):
        out_local(h).wait()
        for peer in peers:
            out_send(h, me, peer).wait_recv()
        incoming = arrived[h].reshape(owners * slots, lanes)
        gathered[h, :, lane_block(my_head)] = dot32(place_hot[...], incoming).astype(
            jnp.bfloat16
        )
        head_send(h, my_head, cross, cross_s, cross_r).start()
        head_send(h, my_head, sibling, sib_s, sib_r).start()

    def relay(h):
        head_send(h, cross, cross, cross_s, cross_r).wait_recv()
        head_send(h, cross, sibling, relay_s, relay_r).start()

    width = out_ref.shape[1]
    tile = 256

    def project(h, final):
        head_send(h, sibling, sibling, sib_s, sib_r).wait_recv()
        head_send(h, diagonal, sibling, relay_s, relay_r).wait_recv()

        def columns_of(index, carry):
            columns = pl.ds(pl.multiple_of(index * tile, tile), tile)
            right = weights[h, :, :, columns].reshape(4 * lanes, tile)
            summed = total[:, columns] + dot32(gathered[h], right)
            if final:
                out_ref[:, columns] = summed.astype(out_ref.dtype)
            else:
                total[:, columns] = summed
            return carry

        lax.fori_loop(0, width // tile, columns_of, 0)

    for h in range(heads):
        weight_load(h).wait()

    place(0)
    place(1)
    relay(0)

    def finish_pair(p, carry):
        place(2 * p)
        relay(2 * p - 1)
        project(2 * p - 2, False)
        place(2 * p + 1)
        relay(2 * p)
        project(2 * p - 1, False)
        return carry

    lax.fori_loop(1, pairs, finish_pair, 0)
    relay(heads - 1)
    project(heads - 2, False)
    project(heads - 1, True)

    for peer in peers:
        pos_send(peer, me).wait_send()
        decay_send(peer, me).wait_send()

    def drain(h, carry):
        raw_send(h, 0, far, me).wait_send()

        @pl.when(outer)
        def _():
            raw_send(h, 1, near, me).wait_send()

        @pl.when(inner)
        def _():
            merged_send(h).wait_send()

        for peer in peers:
            out_send(h, peer, me).wait_send()
        head_send(h, my_head, cross, cross_s, cross_r).wait_send()
        head_send(h, my_head, sibling, sib_s, sib_r).wait_send()
        head_send(h, cross, sibling, relay_s, relay_r).wait_send()
        return carry

    lax.fori_loop(0, heads, drain, 0)


def fused_form(
    queries, keys, values, log_decay, arrival_positions, prompt_lengths, norm_gain, out_weight
):
    rows = queries.shape[0]
    heads = log_decay.shape[1]
    lanes = queries.shape[1] // heads
    owners = lax.axis_size("ctx")
    columns = lax.axis_size("head")
    tokens = owners * rows
    slots = 3 * (rows // (2 * owners))
    pairs = heads // 2
    wide = 2 * lanes
    padded = owners * slots
    features, width = out_weight.shape
    gain = norm_gain.reshape(heads, lanes)
    stacked = out_weight.reshape(columns, heads, lanes, width)
    vmem = pl.BlockSpec(memory_space=pltpu.VMEM)
    anywhere = pl.BlockSpec(memory_space=pl.ANY)
    dma = pltpu.SemaphoreType.DMA
    bf16, f32 = jnp.bfloat16, jnp.float32
    return pl.pallas_call(
        functools.partial(
            state_kernel, owners, rows, heads, lanes, slots, prompt_lengths.shape[0]
        ),
        out_shape=jax.ShapeDtypeStruct((rows, width), bf16),
        in_specs=[
            pl.BlockSpec(memory_space=pltpu.SMEM),
            vmem,
            vmem,
            vmem,
            anywhere,
            anywhere,
            anywhere,
            anywhere,
        ],
        out_specs=vmem,
        scratch_shapes=[
            pltpu.VMEM((1, tokens), jnp.int32),
            pltpu.VMEM((heads, tokens), bf16),
            pltpu.VMEM((3, pairs, rows, wide), bf16),
            pltpu.VMEM((3, pairs, padded, wide), bf16),
            pltpu.VMEM((padded, rows), bf16),
            pltpu.VMEM((rows, padded), bf16),
            pltpu.VMEM((owners, slots, slots), f32),
            pltpu.VMEM((pairs, owners, slots, 2), f32),
            pltpu.VMEM((owners, heads, slots), f32),
            pltpu.VMEM((pairs, owners, slots, 2), f32),
            pltpu.VMEM((pairs, owners, slots, 2), f32),
            pltpu.VMEM((8 * owners, lanes), f32),
            pltpu.VMEM((8 * owners, lanes), f32),
            pltpu.VMEM((heads, 2 * owners, 8 * owners, lanes), f32),
            pltpu.VMEM((owners, heads, owners, lanes, lanes), bf16),
            pltpu.VMEM((heads, owners, lanes, lanes), bf16),
            pltpu.VMEM((heads, owners, lanes, lanes), bf16),
            pltpu.VMEM((owners, lanes, lanes), bf16),
            pltpu.VMEM((heads, owners, slots, lanes), bf16),
            pltpu.VMEM((heads, owners, slots, lanes), bf16),
            pltpu.VMEM((heads, rows, columns * lanes), bf16),
            pltpu.VMEM((heads, columns, lanes, width), bf16),
            pltpu.VMEM((rows, width), f32),
            dma((2,)),
            dma((2, owners)),
            dma((2, owners)),
            dma((3, pairs)),
            dma((heads,)),
            dma((2, heads)),
            dma((owners, heads)),
            dma((heads,)),
            dma((heads,)),
            dma((heads,)),
            dma((owners, heads)),
            dma((owners, heads)),
            dma((heads,)),
            dma((heads,)),
            dma((heads,)),
            dma((heads,)),
            dma((heads,)),
            dma((heads,)),
        ],
        compiler_params=pltpu.CompilerParams(
            collective_id=0, has_side_effects=True, vmem_limit_bytes=58 * 1024 * 1024
        ),
    )(
        prompt_lengths,
        arrival_positions.reshape(1, rows),
        log_decay.T,
        gain,
        queries,
        keys,
        values,
        stacked,
    )


def local(*arguments):
    queries, log_decay = arguments[0], arguments[3]
    fits = (
        log_decay.shape[1] == 8
        and lax.axis_size("ctx") == 4
        and lax.axis_size("head") == 4
        and queries.shape[0] == 512
        and queries.shape[1] == 128 * log_decay.shape[1]
    )
    return (fused_form if fits else exchange_form)(*arguments)


def solution(mesh):
    return jax.shard_map(
        local,
        mesh=mesh,
        in_specs=(
            P(("groups", "ctx"), "head"),
            P(("groups", "ctx"), "head"),
            P(("groups", "ctx"), "head"),
            P(("groups", "ctx"), "head"),
            P(("groups", "ctx")),
            P("groups"),
            P("head"),
            P(None, "head"),
        ),
        out_specs=P(("groups", "ctx"), "head"),
        check_vma=False,
    )
```

```python
import functools

import jax
import jax.numpy as jnp
from jax import lax
from jax.experimental import pallas as pl
from jax.experimental.pallas import tpu as pltpu
from jax.sharding import PartitionSpec as P


def split_terms(source):
    upper_part = source.astype(jnp.bfloat16)
    lower_part = (source - upper_part.astype(jnp.float32)).astype(jnp.bfloat16)
    return (upper_part, lower_part)


def paired_einsum(form, wide_operand, narrow_operand, wide_first):
    upper_part, lower_part = split_terms(wide_operand)
    if wide_first:
        return jnp.einsum(
            form, upper_part, narrow_operand, preferred_element_type=jnp.float32
        ) + jnp.einsum(form, lower_part, narrow_operand, preferred_element_type=jnp.float32)
    return jnp.einsum(
        form, narrow_operand, upper_part, preferred_element_type=jnp.float32
    ) + jnp.einsum(form, narrow_operand, lower_part, preferred_element_type=jnp.float32)


def block_terms(run_state, last_seg, block_q, block_k, block_v, block_cum, block_seg):
    linked = block_seg == last_seg
    reach_back = jnp.where(linked[:, None], jnp.exp(block_cum), 0.0)
    earlier = paired_einsum("thd,hde->the", run_state, block_q, False) * reach_back[:, :, None]
    block_rows = block_seg.shape[0]
    order_ok = jnp.arange(block_rows)[:, None] >= jnp.arange(block_rows)[None, :]
    allowed = order_ok & (block_seg[:, None] == block_seg[None, :])
    by_head = block_cum.T
    spread = by_head[:, :, None] - by_head[:, None, :]
    decay_table = jnp.where(allowed[None], jnp.exp(jnp.where(allowed[None], spread, 0.0)), 0.0)
    scores = jnp.einsum("thd,shd->hts", block_q, block_k, preferred_element_type=jnp.float32)
    inside = paired_einsum("hts,shd->thd", scores * decay_table, block_v, True)
    end_seg = block_seg[-1]
    toward = jnp.where(
        (block_seg == end_seg)[:, None], jnp.exp(block_cum[-1][None, :] - block_cum), 0.0
    )
    local_state = paired_einsum(
        "shd,she->hde", block_k.astype(jnp.float32) * toward[:, :, None], block_v, True
    )
    keep_factor = jnp.where(jnp.all(linked), jnp.exp(block_cum[-1]), 0.0)
    new_state = keep_factor[:, None, None] * run_state + local_state
    return (earlier + inside, new_state)


def attend(own_q, own_k, own_v, cumulative, segment, run_state, last_seg):
    block_out, run_state = block_terms(
        run_state, last_seg, own_q, own_k, own_v, cumulative, segment
    )
    return (block_out, run_state)


def carried_state(factor, end_state):
    owner_count = lax.axis_size("ctx")
    my_index = lax.axis_index("ctx")
    factors, states = (
        lax.all_gather(factor[None].astype(jnp.bfloat16), "ctx", axis=0, tiled=True).astype(
            jnp.float32
        ),
        lax.all_gather(end_state[None].astype(jnp.bfloat16), "ctx", axis=0, tiled=True).astype(
            jnp.float32
        ),
    )
    index_line = jnp.arange(owner_count)
    between = (index_line[None, :] > index_line[:, None]) & (index_line[None, :] < my_index)
    chain_weights = jnp.prod(jnp.where(between[:, :, None], factors[None, :, :], 1.0), axis=1)
    chain_weights = chain_weights * (index_line < my_index)[:, None].astype(jnp.float32)
    return jnp.einsum("nh,nhde->hde", chain_weights, states, precision=lax.Precision.HIGHEST)


def exchange_form(
    queries, keys, values, log_decay, arrival_positions, prompt_lengths, norm_gain, out_weight
):
    row_count = queries.shape[0]
    heads_here = log_decay.shape[1]
    head_width = queries.shape[1] // heads_here
    owner_count = lax.axis_size("ctx")
    my_index = lax.axis_index("ctx")
    capacity = 3 * (row_count // (2 * owner_count))
    slot_total = owner_count * capacity
    every_position = lax.all_gather(arrival_positions, "ctx", axis=0, tiled=True)
    target = arrival_positions // row_count
    hit_table = (target[:, None] == jnp.arange(owner_count)[None, :]).astype(jnp.int32)
    slot_index = jnp.sum((jnp.cumsum(hit_table, axis=0) - 1) * hit_table, axis=1)
    send_slot = target * capacity + slot_index
    send_onehot = (jnp.arange(slot_total)[:, None] == send_slot[None, :]).astype(jnp.bfloat16)

    def pack_rows(source):
        packed = jnp.dot(send_onehot, source, preferred_element_type=jnp.float32).astype(
            source.dtype
        )
        return packed.reshape(owner_count, capacity, source.shape[1])

    arrived = (
        lax.all_to_all(pack_rows(queries), "ctx", split_axis=0, concat_axis=0, tiled=True),
        lax.all_to_all(pack_rows(keys), "ctx", split_axis=0, concat_axis=0, tiled=True),
        lax.all_to_all(pack_rows(values), "ctx", split_axis=0, concat_axis=0, tiled=True),
        lax.all_to_all(pack_rows(log_decay), "ctx", split_axis=0, concat_axis=0, tiled=True),
    )
    layout = every_position.reshape(owner_count, row_count)
    own_rows = layout // row_count == my_index
    rank_index = jnp.cumsum(own_rows.astype(jnp.int32), axis=1) - 1
    source_slot = (jnp.arange(owner_count)[:, None] * capacity + rank_index).reshape(-1)
    wanted = my_index * row_count + jnp.arange(row_count, dtype=jnp.int32)
    matches = every_position[None, :] == wanted[:, None]
    slot_of_row = jnp.sum(jnp.where(matches, source_slot[None, :], 0), axis=1)
    receive_onehot = (slot_of_row[:, None] == jnp.arange(slot_total)[None, :]).astype(jnp.bfloat16)

    def unpack_rows(buffer):
        flat_buffer = buffer.reshape(slot_total, buffer.shape[2])
        return jnp.dot(receive_onehot, flat_buffer, preferred_element_type=jnp.float32).astype(
            buffer.dtype
        )

    own_q = unpack_rows(arrived[0]).reshape(row_count, heads_here, head_width)
    own_k = unpack_rows(arrived[1]).reshape(row_count, heads_here, head_width)
    own_v = unpack_rows(arrived[2]).reshape(row_count, heads_here, head_width)
    cumulative = jnp.cumsum(unpack_rows(arrived[3]).astype(jnp.float32), axis=0)
    positions = my_index * row_count + jnp.arange(row_count, dtype=jnp.int32)
    prompt_ends = jnp.cumsum(prompt_lengths)[:-1]
    segment = jnp.sum((positions[:, None] >= prompt_ends[None, :]).astype(jnp.int32), axis=1)
    opens_prompt = (positions[0] == 0) | jnp.any(positions[0] == prompt_ends)
    through = jnp.logical_not(opens_prompt) & jnp.all(segment == segment[0])
    factor = jnp.where(through, jnp.exp(cumulative[-1]), 0.0)
    entry_seg = jnp.where(opens_prompt, -1, segment[0])
    empty_state = jnp.zeros((heads_here, head_width, head_width), jnp.float32)
    attention, end_state = attend(
        own_q, own_k, own_v, cumulative, segment, empty_state, jnp.int32(-1)
    )
    incoming = carried_state(factor, end_state)
    reach_back = jnp.where((segment == entry_seg)[:, None], jnp.exp(cumulative), 0.0)
    attention = (
        attention + paired_einsum("thd,hde->the", incoming, own_q, False) * reach_back[:, :, None]
    )
    inv_scale = lax.rsqrt(jnp.mean(attention * attention, axis=-1, keepdims=True) + 1e-06)
    normed = (attention * inv_scale * norm_gain.reshape(heads_here, head_width)).astype(
        jnp.bfloat16
    )
    normed = normed.reshape(row_count, heads_here * head_width)
    projected = jnp.dot(
        lax.all_gather(normed, "head", axis=1, tiled=True),
        out_weight,
        preferred_element_type=jnp.float32,
    )
    return projected.astype(jnp.bfloat16)


MESH = pl.DeviceIdType.MESH
NT = (((1,), (1,)), ((), ()))
TN = (((0,), (0,)), ((), ()))
STRIPE = 32


def dot32(left, right, dims=(((1,), (0,)), ((), ()))):
    return lax.dot_general(left, right, dims, preferred_element_type=jnp.float32)


def state_kernel(
    owners,
    rows,
    heads,
    lanes,
    slots,
    prompts,
    lengths_ref,
    pos_ref,
    decay_ref,
    gain_ref,
    q_ref,
    k_ref,
    v_ref,
    w_ref,
    out_ref,
    all_pos,
    all_decay,
    raw_in,
    ordered,
    sort_hot,
    place_hot,
    mask_bias,
    cum_col,
    cum_row,
    toward_col,
    reach_col,
    first_row,
    last_row,
    factor,
    states,
    merged,
    merged_in,
    prefix,
    normed,
    arrived,
    gathered,
    weights,
    total,
    meta_l,
    meta_s,
    meta_r,
    in_l,
    w_l,
    raw_s,
    raw_r,
    merged_s,
    merged_r,
    out_l,
    out_s,
    out_r,
    sib_s,
    sib_r,
    cross_s,
    cross_r,
    relay_s,
    relay_r,
    result,
    result_s,
):
    me = lax.axis_index("ctx")
    my_head = lax.axis_index("head")
    sibling = my_head + 1 - 2 * lax.rem(my_head, 2)
    cross = lax.rem(my_head + 2, 4)
    diagonal = lax.rem(sibling + 2, 4)
    tokens = owners * rows
    pairs = heads // 2
    wide = 2 * lanes
    left_side = me < 2
    peers = [
        jnp.where(left_side, 3, 0),
        jnp.where(left_side, 2, 1),
        me + 1 - 2 * lax.rem(me, 2),
    ]
    far = jnp.where(me < 2, 2, 1)
    near = 3 - far
    edge = jnp.where(me < 2, 0, 3)
    inner = jnp.logical_or(me == 1, me == 2)
    outer = jnp.logical_not(inner)
    sources = (q_ref, k_ref, v_ref)

    def pair_block(index):
        return pl.ds(pl.multiple_of(index * wide, wide), wide)

    def lane_block(index):
        return pl.ds(pl.multiple_of(index * lanes, lanes), lanes)

    def token_block(index):
        return pl.ds(pl.multiple_of(index * rows, rows), rows)

    def in_local(a, p):
        return pltpu.make_async_copy(
            sources[a].at[:, pair_block(p)], raw_in.at[a, p], in_l.at[a, p]
        )

    def weight_load(h):
        return pltpu.make_async_copy(w_ref.at[:, h], weights.at[h], w_l.at[h])

    for p in range(pairs):
        for a in (1, 2):
            in_local(a, p).start()
    for p in range(pairs):
        in_local(0, p).start()

    barrier = pltpu.get_barrier_semaphore()
    for peer in peers:
        pl.semaphore_signal(barrier, inc=1, device_id={"ctx": peer}, device_id_type=MESH)
    for peer in (sibling, cross):
        pl.semaphore_signal(barrier, inc=1, device_id={"head": peer}, device_id_type=MESH)

    def remote(source, target, send, recv, axis, device):
        return pltpu.make_async_remote_copy(
            src_ref=source,
            dst_ref=target,
            send_sem=send,
            recv_sem=recv,
            device_id={axis: device},
            device_id_type=MESH,
        )

    def pos_send(peer, source):
        return remote(
            pos_ref,
            all_pos.at[:, token_block(source)],
            meta_s.at[0, peer],
            meta_r.at[0, source],
            "ctx",
            peer,
        )

    def decay_send(peer, source):
        return remote(
            decay_ref,
            all_decay.at[:, token_block(source)],
            meta_s.at[1, peer],
            meta_r.at[1, source],
            "ctx",
            peer,
        )

    def raw_send(h, slot, peer, source):
        return remote(
            states.at[source, h],
            states.at[source, h],
            raw_s.at[slot, h],
            raw_r.at[source, h],
            "ctx",
            peer,
        )

    def merged_send(h):
        return remote(
            merged.at[h], merged_in.at[h], merged_s.at[h], merged_r.at[h], "ctx", edge
        )

    def out_send(h, owner, source):
        return remote(
            normed.at[h, owner],
            arrived.at[h, source],
            out_s.at[owner, h],
            out_r.at[source, h],
            "ctx",
            owner,
        )

    def out_local(h):
        return pltpu.make_async_copy(normed.at[h, me], arrived.at[h, me], out_l.at[h])

    def head_send(h, head_index, target, send, recv):
        piece = gathered.at[h, :, lane_block(head_index)]
        return remote(piece, piece, send.at[h], recv.at[h], "head", target)

    pos_local = pltpu.make_async_copy(pos_ref, all_pos.at[:, token_block(me)], meta_l.at[0])
    decay_local = pltpu.make_async_copy(
        decay_ref, all_decay.at[:, token_block(me)], meta_l.at[1]
    )
    pos_local.start()
    decay_local.start()
    for h in range(heads):
        weight_load(h).start()

    ends = []
    running = lengths_ref[0]
    for index in range(1, prompts):
        ends.append(running)
        running = running + lengths_ref[index]

    def segment_of(position):
        found = jnp.zeros_like(position)
        for end in ends:
            found = found + jnp.where(position >= end, 1, 0)
        return found

    own_pos = pos_ref[...].astype(jnp.float32)
    decay = decay_ref[...]
    slot_col = lax.broadcasted_iota(jnp.int32, (slots, 1), 0)
    slot_row = lax.broadcasted_iota(jnp.int32, (1, slots), 1)
    later = lax.broadcasted_iota(jnp.int32, (slots, slots), 0)
    sooner = lax.broadcasted_iota(jnp.int32, (slots, slots), 1)
    causal = later >= sooner
    lower = jnp.where(causal, 1.0, 0.0).astype(jnp.bfloat16)
    bounds = []
    for o in range(owners):
        inside = (own_pos >= o * rows) & (own_pos < (o + 1) * rows)
        first = jnp.min(jnp.where(inside, own_pos, 1.0 * tokens), axis=1, keepdims=True)
        last = jnp.max(jnp.where(inside, own_pos, -1.0), axis=1, keepdims=True)
        first_at = first.astype(jnp.int32)
        last_at = last.astype(jnp.int32)
        bounds.append((first_at, last_at))
        here_col = first_at + slot_col
        wanted = jnp.where(here_col <= last_at, here_col, -1).astype(jnp.float32)
        hits = jnp.where(own_pos == wanted, 1.0, 0.0).astype(jnp.bfloat16)
        sort_hot[pl.ds(o * slots, slots), :] = hits
        decay_cols = dot32(hits, decay, NT).astype(jnp.bfloat16)
        col_sums = dot32(lower, decay_cols)
        toward = jnp.where(
            segment_of(here_col) == segment_of(last_at),
            jnp.exp(col_sums[slots - 1 :, :] - col_sums),
            0.0,
        )
        for p in range(pairs):
            cum_col[p, o] = col_sums[:, 2 * p : 2 * p + 2]
            toward_col[p, o] = toward[:, 2 * p : 2 * p + 2]

    pl.semaphore_wait(barrier, owners + 1)
    for peer in peers:
        pos_send(peer, me).start()
        decay_send(peer, me).start()

    half = owners * slots // 2

    def sort_rows(a, p):
        in_local(a, p).wait()
        for part in range(2):
            block = pl.ds(part * half, half)
            ordered[a, p, block, :] = dot32(sort_hot[block, :], raw_in[a, p]).astype(
                jnp.bfloat16
            )

    def make_states(p, carry):
        sort_rows(1, p)
        sort_rows(2, p)
        for j in range(2):
            h = 2 * p + j
            for o in range(owners):
                run = pl.ds(o * slots, slots)
                side = slice(j * lanes, (j + 1) * lanes)
                key = ordered[1, p, run, side]
                value = ordered[2, p, run, side]
                weighted = key.astype(jnp.float32) * toward_col[p, o][:, j : j + 1]
                states[me, h, o] = dot32(weighted.astype(jnp.bfloat16), value, TN).astype(
                    jnp.bfloat16
                )
            raw_send(h, 0, far, me).start()

            @pl.when(outer)
            def _():
                raw_send(h, 1, near, me).start()

        return carry

    lax.fori_loop(0, pairs, make_states, 0)

    for o in range(owners):
        first_at, last_at = bounds[o]
        hits = sort_hot[pl.ds(o * slots, slots), :]
        decay_rows = dot32(decay, hits, NT).astype(jnp.bfloat16)
        cum_row[o] = dot32(decay_rows, lower, NT)
        seg_col = segment_of(first_at + slot_col)
        seg_row = segment_of(first_at + slot_row)
        seg_first = segment_of(first_at)
        mask_bias[o] = jnp.where(causal & (seg_col == seg_row), 0.0, -1e30)
        for p in range(pairs):
            reach_col[p, o] = jnp.where(seg_col == seg_first, jnp.exp(cum_col[p, o]), 0.0)

    def sort_queries(p, carry):
        sort_rows(0, p)
        return carry

    lax.fori_loop(0, pairs, sort_queries, 0)

    pos_local.wait()
    decay_local.wait()
    for peer in peers:
        pos_send(me, peer).wait_recv()
        decay_send(me, peer).wait_recv()

    group_iota = lax.broadcasted_iota(jnp.int32, (8, rows), 0).astype(jnp.float32) * rows
    for d in range(owners):
        held = all_pos[:, d * rows : (d + 1) * rows].astype(jnp.float32)
        inside = (held >= group_iota) & (held < group_iota + rows)
        first = jnp.min(jnp.where(inside, held, 1.0 * tokens), axis=1, keepdims=True)
        last = jnp.max(jnp.where(inside, held, -1.0), axis=1, keepdims=True)
        first_row[d * 8 : d * 8 + 8, :] = jnp.broadcast_to(first, (8, lanes))
        last_row[d * 8 : d * 8 + 8, :] = jnp.broadcast_to(last, (8, lanes))

    every_pos = all_pos[...].astype(jnp.float32)
    every_decay = all_decay[...]
    last_all = last_row[...][:, :1]
    seg_all = segment_of(last_all.astype(jnp.int32))
    holder = lax.broadcasted_iota(jnp.int32, (8 * owners, 1), 0) // 8
    for t in range(2 * owners):
        device = me if t < owners else edge
        start = first_row[pl.ds(device * 8 + t % owners, 1), :][:, :1]
        between = (every_pos > last_all) & (every_pos < start)
        sums = dot32(jnp.where(between, 1.0, 0.0).astype(jnp.bfloat16), every_decay, NT)
        linked = (last_all < start) & (seg_all == segment_of(start.astype(jnp.int32)))
        if t >= owners:
            linked = linked & (holder != edge)
        scale = jnp.where(linked, jnp.exp(sums), 0.0)
        for h in range(heads):
            factor[h, t] = jnp.broadcast_to(scale[:, h : h + 1], (8 * owners, lanes))

    line = lax.broadcasted_iota(jnp.int32, (1, owners * slots), 1).astype(jnp.float32)
    source_pos = jnp.full((1, owners * slots), -1.0, jnp.float32)
    for d in range(owners):
        first = first_row[pl.ds(d * 8 + me, 1), :][:, :1]
        last = last_row[pl.ds(d * 8 + me, 1), :][:, :1]
        found = first + (line - 1.0 * d * slots)
        fine = (line >= d * slots) & (line < (d + 1) * slots) & (found <= last)
        source_pos = jnp.where(fine, found, source_pos)
    target_pos = (me * rows + lax.broadcasted_iota(jnp.int32, (rows, 1), 0)).astype(jnp.float32)
    place_hot[...] = jnp.where(target_pos == source_pos, 1.0, 0.0).astype(jnp.bfloat16)
    total[...] = jnp.zeros_like(total)

    def stripe(index):
        return pl.ds(pl.multiple_of(index * STRIPE, STRIPE), STRIPE)

    def merge_inner(h):
        def body(index, carry):
            block = stripe(index)
            sums = [None] * (2 * owners)
            for d in range(owners):
                for past in range(owners):
                    tile = states[d, h, past, block, :].astype(jnp.float32)
                    for t in range(2 * owners):
                        if past <= t % owners:
                            term = tile * factor[h, t, pl.ds(d * 8 + past, 1), :]
                            sums[t] = term if sums[t] is None else sums[t] + term
            for o in range(owners):
                prefix[o, block, :] = sums[o].astype(jnp.bfloat16)
                merged[h, o, block, :] = sums[owners + o].astype(jnp.bfloat16)
            return carry

        lax.fori_loop(0, lanes // STRIPE, body, 0)

    def merge_outer(h):
        def body(index, carry):
            block = stripe(index)
            for o in range(owners):
                summed = merged_in[h, o, block, :].astype(jnp.float32)
                for past in range(o):
                    tile = states[me, h, past, block, :].astype(jnp.float32)
                    summed = summed + tile * factor[h, o, pl.ds(me * 8 + past, 1), :]
                prefix[o, block, :] = summed.astype(jnp.bfloat16)
            return carry

        lax.fori_loop(0, lanes // STRIPE, body, 0)

    def attend_pair(p, carry):
        for j in range(2):
            h = 2 * p + j

            @pl.when(inner)
            def _():
                for peer in peers:
                    raw_send(h, 0, me, peer).wait_recv()
                merge_inner(h)
                merged_send(h).start()

            @pl.when(outer)
            def _():
                merged_send(h).wait_recv()
                merge_outer(h)

            gain = gain_ref[pl.ds(h, 1), :]
            for o in range(owners):
                run = pl.ds(o * slots, slots)
                side = slice(j * lanes, (j + 1) * lanes)
                query = ordered[0, p, run, side]
                key = ordered[1, p, run, side]
                value = ordered[2, p, run, side]
                col = cum_col[p, o][:, j : j + 1]
                row = cum_row[o, pl.ds(h, 1), :]
                table = jnp.exp(col - row + mask_bias[o])
                scores = (dot32(query, key, NT) * table).astype(jnp.bfloat16)
                result = dot32(scores, value)
                result = result + dot32(query, prefix[o]) * reach_col[p, o][:, j : j + 1]
                scale = lax.rsqrt(jnp.mean(result * result, axis=-1, keepdims=True) + 1e-06)
                normed[h, o] = (result * scale * gain).astype(jnp.bfloat16)
            for peer in peers:
                out_send(h, peer, me).start()
            out_local(h).start()
        return carry

    lax.fori_loop(0, pairs, attend_pair, 0)

    def place(h):
        out_local(h).wait()
        for peer in peers:
            out_send(h, me, peer).wait_recv()
        incoming = arrived[h].reshape(owners * slots, lanes)
        gathered[h, :, lane_block(my_head)] = dot32(place_hot[...], incoming).astype(
            jnp.bfloat16
        )
        head_send(h, my_head, cross, cross_s, cross_r).start()
        head_send(h, my_head, sibling, sib_s, sib_r).start()

    def relay(h):
        head_send(h, cross, cross, cross_s, cross_r).wait_recv()
        head_send(h, cross, sibling, relay_s, relay_r).start()

    width = out_ref.shape[1]
    tile = 768

    def store(index):
        columns = pl.ds(pl.multiple_of(index * tile, tile), tile)
        return pltpu.make_async_copy(
            result.at[:, columns], out_ref.at[:, columns], result_s.at[index]
        )

    def project(h, final):
        head_send(h, sibling, sibling, sib_s, sib_r).wait_recv()
        head_send(h, diagonal, sibling, relay_s, relay_r).wait_recv()

        def columns_of(index, carry):
            columns = pl.ds(pl.multiple_of(index * tile, tile), tile)
            right = weights[h, :, :, columns].reshape(4 * lanes, tile)
            summed = total[:, columns] + dot32(gathered[h], right)
            if final:
                result[:, columns] = summed.astype(out_ref.dtype)
                store(index).start()
            else:
                total[:, columns] = summed
            return carry

        lax.fori_loop(0, width // tile, columns_of, 0)

    for h in range(heads):
        weight_load(h).wait()

    place(0)
    place(1)
    relay(0)

    def finish_pair(p, carry):
        place(2 * p)
        relay(2 * p - 1)
        project(2 * p - 2, False)
        place(2 * p + 1)
        relay(2 * p)
        project(2 * p - 1, False)
        return carry

    lax.fori_loop(1, pairs, finish_pair, 0)
    relay(heads - 1)
    project(heads - 2, False)
    project(heads - 1, True)

    for peer in peers:
        pos_send(peer, me).wait_send()
        decay_send(peer, me).wait_send()

    def drain(h, carry):
        raw_send(h, 0, far, me).wait_send()

        @pl.when(outer)
        def _():
            raw_send(h, 1, near, me).wait_send()

        @pl.when(inner)
        def _():
            merged_send(h).wait_send()

        for peer in peers:
            out_send(h, peer, me).wait_send()
        head_send(h, my_head, cross, cross_s, cross_r).wait_send()
        head_send(h, my_head, sibling, sib_s, sib_r).wait_send()
        head_send(h, cross, sibling, relay_s, relay_r).wait_send()
        return carry

    lax.fori_loop(0, heads, drain, 0)
    for index in range(width // tile):
        store(index).wait()


def fused_form(
    queries, keys, values, log_decay, arrival_positions, prompt_lengths, norm_gain, out_weight
):
    rows = queries.shape[0]
    heads = log_decay.shape[1]
    lanes = queries.shape[1] // heads
    owners = lax.axis_size("ctx")
    columns = lax.axis_size("head")
    tokens = owners * rows
    slots = 3 * (rows // (2 * owners))
    pairs = heads // 2
    wide = 2 * lanes
    padded = owners * slots
    features, width = out_weight.shape
    gain = norm_gain.reshape(heads, lanes)
    stacked = out_weight.reshape(columns, heads, lanes, width)
    vmem = pl.BlockSpec(memory_space=pltpu.VMEM)
    anywhere = pl.BlockSpec(memory_space=pl.ANY)
    dma = pltpu.SemaphoreType.DMA
    bf16, f32 = jnp.bfloat16, jnp.float32
    return pl.pallas_call(
        functools.partial(
            state_kernel, owners, rows, heads, lanes, slots, prompt_lengths.shape[0]
        ),
        out_shape=jax.ShapeDtypeStruct((rows, width), bf16),
        in_specs=[
            pl.BlockSpec(memory_space=pltpu.SMEM),
            vmem,
            vmem,
            vmem,
            anywhere,
            anywhere,
            anywhere,
            anywhere,
        ],
        out_specs=anywhere,
        scratch_shapes=[
            pltpu.VMEM((1, tokens), jnp.int32),
            pltpu.VMEM((heads, tokens), bf16),
            pltpu.VMEM((3, pairs, rows, wide), bf16),
            pltpu.VMEM((3, pairs, padded, wide), bf16),
            pltpu.VMEM((padded, rows), bf16),
            pltpu.VMEM((rows, padded), bf16),
            pltpu.VMEM((owners, slots, slots), f32),
            pltpu.VMEM((pairs, owners, slots, 2), f32),
            pltpu.VMEM((owners, heads, slots), f32),
            pltpu.VMEM((pairs, owners, slots, 2), f32),
            pltpu.VMEM((pairs, owners, slots, 2), f32),
            pltpu.VMEM((8 * owners, lanes), f32),
            pltpu.VMEM((8 * owners, lanes), f32),
            pltpu.VMEM((heads, 2 * owners, 8 * owners, lanes), f32),
            pltpu.VMEM((owners, heads, owners, lanes, lanes), bf16),
            pltpu.VMEM((heads, owners, lanes, lanes), bf16),
            pltpu.VMEM((heads, owners, lanes, lanes), bf16),
            pltpu.VMEM((owners, lanes, lanes), bf16),
            pltpu.VMEM((heads, owners, slots, lanes), bf16),
            pltpu.VMEM((heads, owners, slots, lanes), bf16),
            pltpu.VMEM((heads, rows, columns * lanes), bf16),
            pltpu.VMEM((heads, columns, lanes, width), bf16),
            pltpu.VMEM((rows, width), f32),
            dma((2,)),
            dma((2, owners)),
            dma((2, owners)),
            dma((3, pairs)),
            dma((heads,)),
            dma((2, heads)),
            dma((owners, heads)),
            dma((heads,)),
            dma((heads,)),
            dma((heads,)),
            dma((owners, heads)),
            dma((owners, heads)),
            dma((heads,)),
            dma((heads,)),
            dma((heads,)),
            dma((heads,)),
            dma((heads,)),
            dma((heads,)),
            pltpu.VMEM((rows, width), bf16),
            dma((width // 768,)),
        ],
        compiler_params=pltpu.CompilerParams(
            collective_id=0, has_side_effects=True, vmem_limit_bytes=58 * 1024 * 1024
        ),
    )(
        prompt_lengths,
        arrival_positions.reshape(1, rows),
        log_decay.T,
        gain,
        queries,
        keys,
        values,
        stacked,
    )


def local(*arguments):
    queries, log_decay = arguments[0], arguments[3]
    fits = (
        log_decay.shape[1] == 8
        and lax.axis_size("ctx") == 4
        and lax.axis_size("head") == 4
        and queries.shape[0] == 512
        and queries.shape[1] == 128 * log_decay.shape[1]
    )
    return (fused_form if fits else exchange_form)(*arguments)


def solution(mesh):
    return jax.shard_map(
        local,
        mesh=mesh,
        in_specs=(
            P(("groups", "ctx"), "head"),
            P(("groups", "ctx"), "head"),
            P(("groups", "ctx"), "head"),
            P(("groups", "ctx"), "head"),
            P(("groups", "ctx")),
            P("groups"),
            P("head"),
            P(None, "head"),
        ),
        out_specs=P(("groups", "ctx"), "head"),
        check_vma=False,
    )
```
